128 devices in a mesh: grp: 4 (over z_hi, core), mem: 32 (over x, y, z_lo).
Axes of the slice: x: 4, y: 4, z: 4 (z_hi: 2, z_lo: 2; z = z_hi * 2 + z_lo), core: 2. Of those that a mesh axis runs over, the one named last changes fastest.
Arguments:
- perturb: float32 [128, 1024, 1024], P(('grp', 'mem')), may hold values from -0.1875 to 0.1875
- touched_vertex_index: int32 [128, 4, 64], P(('grp', 'mem')), may hold values from 0 to 1023
- proposed_spin_values: int32 [128, 4, 64], P(('grp', 'mem')), may hold values from 0 to 1
- accept: int32 [128, 4, 64], P(('grp', 'mem')), may hold values 0 or 1
- vertex_site_index: int32 [128, 1024], P(('grp', 'mem')), may hold values from 0 to 63
- vertex_time_index: int32 [128, 1024], P(('grp', 'mem')), may hold values from 0 to 4095
- left_proj: float32 [64, 1024], replicated, may hold values from -0.06 to 0.06
- right_proj: float32 [64, 1024], replicated, may hold values from -0.06 to 0.06
- weights: float32 [128], P(('grp', 'mem')), may hold values from 0.3 to 3
- routing: int32 [128, 1], P(('grp', 'mem')), may hold values from 0 to 31; in each aligned block of 32 rows (0 to 31, 32 to 63, ...) at most 2 rows name the same one
- vertex_function_total: float32 [16, 4096, 4096], P('grp', 'mem'), may hold values from -6 to 6
Outputs:
- four_point_out: float32 [16, 4096, 4096], P('grp', 'mem')
The draws below stay inside these ranges and needn't reach their ends.
Inputs may be any that keep to these rules, and one draw needn't show every extreme that they name: `routing`: among the 32 walkers of one group no member index is named by more than 2 walkers, and in some group one index is named by exactly 2.
All inputs are finite; a program needn't handle non-finite values. No bound on the sum of `accept` on one device may be relied on, other than what follows from the above.
Results may differ from the reference program's by a relative error of at most 0.0003.
Values sent between devices are 32-bit elements; how exact they have to be, the bound alone decides.
No kernel may reach another device: no remote copies, remote signals or barrier semaphores. Data moves between devices by JAX's collectives and lax.ppermute only.
A program may use at most 128 MiB of HBM per device.

```python
import math
import jax
import jax.numpy as jnp
import numpy as np
from jax import lax

K = 1024
SITES = 64
LEG = 64
Q = 16
TIMES = 4096
RANKB = 64
UPDATES = 4
CAP = 2
ORDER = 4096
WALKERS = 128
N_GRP = 4
N_MEM = 32


def place_ends(array, rng, least, top_value):
    index_at = [jax.random.randint(jax.random.fold_in(rng, axis), (), 0, length) for axis, length in enumerate(array.shape)]
    main_axis = array.shape.index(max(array.shape))
    next_to = index_at[:main_axis] + [(index_at[main_axis] + 1) % array.shape[main_axis]] + index_at[main_axis + 1:]
    return array.at[tuple(index_at)].set(least).at[tuple(next_to)].set(top_value)


def shard_levels(rng, shape, cuts, least, largest):
    def one(axis_at, shards_of):
        steps = jax.random.uniform(jax.random.fold_in(jax.random.fold_in(rng, 6), axis_at), (shards_of,), jnp.float32, least / len(cuts), largest / len(cuts))
        return jnp.repeat(jnp.exp(steps), shape[axis_at] // shards_of).reshape((-1,) + (1,) * (len(shape) - axis_at - 1))

    level = one(*cuts[0])
    for cut in cuts[1:]:
        level = level * one(*cut)
    return level


def assign_block(stream_key, own, number, rows, number_of, top, most, skew):
    sequence = jax.random.permutation(stream_key, number_of)
    crowded, common = portions_of(number_of, rows * top, most, skew, True), portions_of(number_of, rows * top, most, skew, False)
    places = jnp.arange(number_of)

    def named(lengths, rotation):
        used = int((lengths > 0).sum())
        fixed = max(1, used // 4)
        passed = fixed + (places - fixed + rotation * (used - fixed)) % max(1, number_of - fixed)
        return jnp.zeros((number_of,), jnp.int32).at[sequence[jnp.where(places < fixed, places, passed)]].set(jnp.asarray(lengths, jnp.int32))

    lengths = jnp.where(number % 4 == 0, named(crowded, number // 4), named(common, number - number // 4 - 1))
    mixed = jax.random.permutation(jax.random.fold_in(own, 3), number_of)
    giver, sink = mixed[0:number_of // 2 * 2:2], mixed[1:number_of // 2 * 2:2]
    slack = jnp.minimum(lengths[giver] - 1, most - lengths[sink]) // 2
    slack = jnp.where((giver == sequence[0]) | (sink == sequence[0]) | (lengths[sink] == 0), 0, jnp.maximum(slack, 0))
    passed = jax.random.randint(jax.random.fold_in(own, 4), (number_of // 2,), 0, 1 << 20) % (slack + 1)
    lengths = lengths.at[giver].add(-passed).at[sink].add(passed)
    items = jnp.searchsorted(jnp.cumsum(lengths), jnp.arange(rows * top), side="right").astype(jnp.int32)
    listing = items.reshape(top, rows).T
    listing = listing[jax.random.permutation(jax.random.fold_in(own, 1), rows)]
    rotation = jax.random.randint(jax.random.fold_in(own, 2), (rows, 1), 0, top)
    return jnp.take_along_axis(listing, (jnp.arange(top)[None, :] + rotation) % top, axis=1)


def portions_of(amount, total, reach, skew, full):
    loads = [(1 << 20) // math.isqrt(rank ** skew) + 1 for rank in range(1, amount + 1)]
    largest = reach if full else min(reach, max(-(-total // amount), total * loads[0] // sum(loads)))
    least = 1 if total - largest >= amount - 1 else 0
    counts, spare = [largest] + [least] * (amount - 1), total - largest - least * (amount - 1)
    while spare > 0:
        candidates = [i for i in range(1, amount) if counts[i] < largest] or [i for i in range(1, amount) if counts[i] < reach]
        whole, left = sum([loads[i] for i in candidates]), spare
        for i in candidates:
            addition = min(reach - counts[i], max(1, left * loads[i] // whole), spare)
            counts[i] = counts[i] + addition
            spare = spare - addition
    return np.array(counts)


def centred(stream_key, dims, scale, reach, cuts=(), kind=jnp.bfloat16):
    array = scale * jax.random.normal(stream_key, dims, jnp.float32)
    if cuts:
        array = array * shard_levels(stream_key, dims, cuts, -0.22, 0.18)
    return jnp.clip(array, -reach, reach).astype(kind)


def setup_inputs(seed: int = 0) -> dict:
    key_list = jax.random.split(jax.random.key(seed), 12)
    perturb = centred(key_list[0], (WALKERS, K, K), K ** -0.5, 0.1875, ((0, 128),), jnp.float32)
    touched_vertex_index = place_ends(jax.random.randint(key_list[1], (WALKERS, UPDATES, RANKB), 0, K), jax.random.fold_in(key_list[1], 1), 0, K - 1).astype(jnp.int32)
    proposed_spin_values = place_ends(jax.random.randint(key_list[2], (WALKERS, UPDATES, RANKB), 0, 2), jax.random.fold_in(key_list[2], 1), 0, 1).astype(jnp.int32)
    accept = place_ends((jax.random.randint(key_list[3], (WALKERS, UPDATES, RANKB), 0, 4) < 3).astype(jnp.int32), jax.random.fold_in(key_list[3], 1), 0, 1)
    vertex_site_index = place_ends(jax.random.randint(key_list[4], (WALKERS, K), 0, SITES), jax.random.fold_in(key_list[4], 1), 0, SITES - 1).astype(jnp.int32)
    vertex_time_index = place_ends(jax.random.randint(key_list[5], (WALKERS, K), 0, TIMES), jax.random.fold_in(key_list[5], 1), 0, TIMES - 1).astype(jnp.int32)
    left_proj = centred(key_list[6], (SITES, LEG * Q), 0.01, 0.06, (), jnp.float32)
    right_proj = centred(key_list[7], (SITES, LEG * Q), 0.01, 0.06, (), jnp.float32)
    weights = jnp.clip(jnp.exp(math.log(3.0) - 2.3025851 * jax.random.uniform(key_list[8], (WALKERS,), jnp.float32) ** shard_levels(key_list[8], (WALKERS,), ((0, 128),), -0.2, 0.2)), 0.3, 3.0)
    routing_keys = jax.random.split(jax.random.fold_in(key_list[9], 1), WALKERS // N_MEM)
    routing_turns = jax.random.permutation(jax.random.fold_in(key_list[9], 3), WALKERS // N_MEM)
    routing = jax.vmap(lambda own, number: assign_block(jax.random.fold_in(key_list[9], 2), own, number, N_MEM, N_MEM, 1, CAP, 2))(routing_keys, routing_turns).reshape((WALKERS, 1))
    vertex_function_total = centred(key_list[10], (Q, ORDER, ORDER), 1.0, 6.0, ((0, 4), (1, 32)), jnp.float32)
    return {"perturb": perturb, "touched_vertex_index": touched_vertex_index, "proposed_spin_values": proposed_spin_values, "accept": accept, "vertex_site_index": vertex_site_index, "vertex_time_index": vertex_time_index, "left_proj": left_proj, "right_proj": right_proj, "weights": weights, "routing": routing, "vertex_function_total": vertex_function_total}


EXACT_ARITHMETIC = lax.Precision.HIGHEST

def legendre(time_ids):
    abscissa = (2.0 * time_ids.astype(jnp.float32) + 1.0) / TIMES - 1.0
    polys = [jnp.ones_like(abscissa), abscissa]
    for degree in range(1, LEG - 1):
        polys.append(((2 * degree + 1) * abscissa * polys[degree] - degree * polys[degree - 1]) / (degree + 1))
    norms = jnp.sqrt(2.0 * jnp.arange(LEG, dtype=jnp.float32) + 1.0)
    return jnp.stack(polys[:LEG], axis=1) * norms[None, :]

def make_onehot(site_ids):
    return (site_ids[:, None] == jnp.arange(SITES, dtype=jnp.int32)[None, :]).astype(jnp.float32)

def project(onehot, polys, table):
    spread = jnp.dot(onehot, table, precision=EXACT_ARITHMETIC, preferred_element_type=jnp.float32)
    return lax.optimization_barrier(jnp.sum(spread.reshape(-1, LEG, Q) * polys[:, :, None], axis=1))

def transform(onehot, polys, values):
    weighted = (polys[:, :, None] * values[:, None, :]).reshape(-1, LEG * Q)
    summed = jnp.dot(onehot.T, weighted, precision=EXACT_ARITHMETIC, preferred_element_type=jnp.float32)
    return summed.reshape(SITES, LEG, Q).transpose(2, 0, 1).reshape(Q, SITES * LEG)

def update_walker(perturb, touched_vertex_index, proposed_spin_values, accept):
    matrix = jnp.eye(K, dtype=jnp.float32) + perturb
    gammas = accept.astype(jnp.float32) * jnp.where(proposed_spin_values == 1, 0.6, -0.4).astype(jnp.float32)
    positions = jnp.arange(K, dtype=jnp.int32)

    def apply_update(update, matrix):
        chosen = touched_vertex_index[update]
        unit_cols = (positions[:, None] == chosen[None, :]).astype(jnp.float32)
        columns = (jnp.take(matrix, chosen, axis=1) - unit_cols) * gammas[update][None, :]
        row_block = jnp.take(matrix, chosen, axis=0)
        return matrix - jnp.dot(columns, row_block, precision=EXACT_ARITHMETIC, preferred_element_type=jnp.float32)
    return lax.fori_loop(0, UPDATES, apply_update, matrix)

def measure_one(perturb, touched_vertex_index, proposed_spin_values, accept, vertex_site_index, vertex_time_index, left_proj, right_proj):
    matrix = update_walker(perturb, touched_vertex_index, proposed_spin_values, accept)
    polys = legendre(vertex_time_index)
    onehot = make_onehot(vertex_site_index)
    left_vec = project(onehot, polys, left_proj)
    right_vec = project(onehot, polys, right_proj)
    left_image = jnp.dot(matrix, left_vec, precision=EXACT_ARITHMETIC, preferred_element_type=jnp.float32)
    right_image = jnp.dot(matrix.T, right_vec, precision=EXACT_ARITHMETIC, preferred_element_type=jnp.float32)
    return (transform(onehot, polys, left_image), transform(onehot, polys, right_image))

def reference(perturb, touched_vertex_index, proposed_spin_values, accept, vertex_site_index, vertex_time_index, left_proj, right_proj, weights, routing, vertex_function_total):

    def single_walker_result(inputs):
        return measure_one(inputs[0], inputs[1], inputs[2], inputs[3], inputs[4], inputs[5], left_proj, right_proj)
    left_observed, right_observed = lax.map(single_walker_result, (perturb, touched_vertex_index, proposed_spin_values, accept, vertex_site_index, vertex_time_index))
    targets = routing[:, 0]
    member_mask = (targets[:, None] == jnp.arange(N_MEM, dtype=jnp.int32)[None, :]).astype(jnp.float32)
    members = member_mask * weights[:, None]
    totals = members.reshape(N_GRP, N_MEM, N_MEM).sum(axis=1)
    group_totals = jnp.repeat(totals, N_MEM, axis=0)
    own_total = lax.optimization_barrier(jnp.sum(group_totals * member_mask, axis=1))
    gamma_factor_list = weights / own_total
    rescaled_rows = left_observed * gamma_factor_list[:, None, None]
    return vertex_function_total + jnp.einsum('npa,npk->pak', rescaled_rows, right_observed, precision=EXACT_ARITHMETIC)
```

```python
import functools

import jax
import jax.numpy as jnp
import numpy as np
from jax import lax
from jax.experimental import pallas as pl
from jax.experimental.pallas import tpu as pltpu
from jax.sharding import Mesh
from jax.sharding import PartitionSpec as P

K = 1024
SITES = 64
LEG = 64
Q = 16
TIMES = 4096
UPDATES = 4
RANKB = 64
NS = UPDATES * RANKB
GQ = 4
RIGHT_ROWS = GQ * 32
LEFT_ROWS = GQ * 16
BLOCK_ROWS = RIGHT_ROWS + LEFT_ROWS + 8
PIECE_ROWS = 4 * RIGHT_ROWS + 8
F32 = jnp.float32
BF16 = jnp.bfloat16
NN = (((1,), (0,)), ((), ()))
NT = (((1,), (1,)), ((), ()))
TN = (((0,), (0,)), ((), ()))
MIB = 1 << 20


def mm(a, b, dims=NN):
    return lax.dot_general(a, b, dims, preferred_element_type=F32)


def split2(x):
    hi = x.astype(BF16)
    return hi, (x - hi.astype(F32)).astype(BF16)


def split3(x):
    hi = x.astype(BF16)
    rest = x - hi.astype(F32)
    mid = rest.astype(BF16)
    return hi, mid, (rest - mid.astype(F32)).astype(BF16)


def mm3(a, b, dims=NN):
    ah, al = a if isinstance(a, tuple) else split2(a)
    bh, bl = b if isinstance(b, tuple) else split2(b)
    return mm(ah, bh, dims) + (mm(al, bh, dims) + mm(ah, bl, dims))


def iota(shape, dim):
    return lax.broadcasted_iota(jnp.int32, shape, dim)


def row_to_column(row):
    n = row.shape[1]
    same = iota((n, n), 0) == iota((n, n), 1)
    return jnp.sum(jnp.where(same, row, jnp.zeros_like(row)), axis=1, keepdims=True)


def measure_kernel(
    place_ref, chosen_ref, gamma_ref, site_ref, time_ref, left_ref, right_ref, weight_ref, key_ref, perturb_ref,
    *rest,
):
    outs = rest[:8]
    (matrix, p_hi, p_lo, polys, spread, vecs, left_meas, right_meas, sem) = rest[8:]
    load = pltpu.make_async_copy(perturb_ref.at[0], matrix, sem)
    load.start()

    abscissa = (2.0 * time_ref[...].astype(F32) + 1.0) / TIMES - 1.0
    before, now = jnp.ones_like(abscissa), abscissa
    polys[0:1, :] = before
    polys[1:2, :] = now * float(np.sqrt(3.0))
    for degree in range(1, LEG - 1):
        after = abscissa * now * ((2 * degree + 1) / (degree + 1)) - before * (degree / (degree + 1))
        before, now = now, after
        polys[degree + 1 : degree + 2, :] = now * float(np.sqrt(2.0 * degree + 3.0))

    sites = site_ref[...]
    onehot = (iota((SITES, K), 0) == sites).astype(F32).astype(BF16)
    onehot3 = jnp.concatenate([onehot, onehot, onehot], axis=0)
    for side, table_ref in ((0, left_ref), (1, right_ref)):
        table = jnp.concatenate(split3(table_ref[...]), axis=0)
        spread[...] = mm(table, onehot3, TN)
        total = jnp.zeros((Q, K), F32)
        for degree in range(LEG):
            total = total + spread[degree * Q : (degree + 1) * Q, :] * polys[degree : degree + 1, :]
        vecs[side] = total

    chosen = row_to_column(chosen_ref[...].astype(F32)).astype(jnp.int32)
    pick = (iota((NS, K), 1) == chosen).astype(F32).astype(BF16)
    gamma = gamma_ref[...]
    load.wait()
    for step in range(4):
        rows = slice(step * 256, (step + 1) * 256)
        hi, lo = split2(matrix[rows, :])
        p_hi[rows, :] = hi
        p_lo[rows, :] = lo
    ph, plo = p_hi[...], p_lo[...]
    v, w = vecs[0], vecs[1]
    wh, wl = split2(w)
    high = mm(jnp.concatenate([pick, wh, wl], axis=0), ph)
    low = mm(jnp.concatenate([pick, wh], axis=0), plo)
    rows_hi, rows_lo = high[:NS].astype(BF16), low[:NS].astype(BF16)
    from_w = high[NS : NS + Q] + high[NS + Q :] + low[NS:]
    same = mm(pick, pick, NT)
    small = mm(rows_hi, pick, NT) + mm(rows_lo, pick, NT)
    vs = split3(v)
    p_vec = (mm(vs[0], pick, NT) + mm(vs[1], pick, NT) + mm(vs[2], pick, NT)) + mm3(
        (vs[0], vs[1]), (rows_hi, rows_lo), NT
    )
    fs = split3(from_w)
    q_vec = mm(fs[0], pick, NT) + mm(fs[1], pick, NT) + mm(fs[2], pick, NT)
    row_block = lax.div(iota((NS, NS), 0), RANKB)
    col_block = lax.div(iota((NS, NS), 1), RANKB)
    c_all, r_all = jnp.zeros((NS, NS), F32), jnp.zeros((NS, NS), F32)
    for update in range(UPDATES):
        columns = jnp.where(col_block == update, small * gamma, 0.0)
        rows_now = small + same
        c_all = c_all + columns
        r_all = jnp.where(row_block == update, rows_now, r_all)
        if update < UPDATES - 1:
            small = small - mm3(columns, rows_now)
    lower = split2(jnp.where(row_block > col_block, c_all, 0.0))
    upper = split2(jnp.where(row_block < col_block, r_all, 0.0))
    x, y = p_vec, q_vec * gamma
    for _ in range(UPDATES - 1):
        x = p_vec - mm3(x, lower, NT)
        y = (q_vec - mm3(y, upper)) * gamma
    z, y2 = x, y
    for _ in range(UPDATES - 1):
        z = x - mm3(z * gamma, upper, NT)
        y2 = y - mm3(y2, lower)
    zs, ys = split3(z * gamma), split3(y2)
    left_arg = v - (mm(zs[0], pick) + mm(zs[1], pick) + mm(zs[2], pick))
    left_image = v + mm3(left_arg, (ph, plo), NT)
    right_arg = w - (mm(ys[0], pick) + mm(ys[1], pick) + mm(ys[2], pick))
    right_image = right_arg + from_w - mm3((ys[0], ys[1]), (rows_hi, rows_lo))

    pol_hi, pol_lo = split2(polys[...])
    both = jnp.concatenate([pol_hi, pol_hi, pol_lo, pol_lo], axis=0)
    even_site = iota((32, K), 0) * 2 == sites
    odd_site = iota((32, K), 0) * 2 + 1 == sites
    first_lanes = iota((64, 128), 1) < LEG
    for image, meas in ((right_image, right_meas), (left_image, left_meas)):
        ih = image.astype(BF16).astype(F32)
        il = image - ih
        for q in range(0, Q, 2):
            def masked(site, part):
                return jnp.concatenate(
                    [jnp.where(site, part[q + k : q + k + 1, :], 0.0).astype(BF16) for k in range(2)], axis=0
                )
            tops = jnp.concatenate([masked(even_site, ih), masked(odd_site, ih)], axis=0)
            bots = jnp.concatenate([masked(even_site, il), masked(odd_site, il)], axis=0)
            high = mm(tops, both, NT)
            low = mm(bots, both[:128], NT)
            whole = high[:, :128] + (high[:, 128:] + low)
            meas[q * 32 : (q + 2) * 32, :] = jnp.where(first_lanes, whole[:64], whole[64:])

    lane = iota((8, 128), 1)
    meta = jnp.where(lane == 0, weight_ref[0], jnp.where(lane == 1, key_ref[0], 0.0))
    for distance in range(8):
        target = place_ref[0] ^ distance
        group, half = target // 2, target % 2
        first = pl.multiple_of(group * RIGHT_ROWS, RIGHT_ROWS)
        outs[distance][0:RIGHT_ROWS, :] = right_meas[pl.ds(first, RIGHT_ROWS), :]
        outs[distance][RIGHT_ROWS : RIGHT_ROWS + LEFT_ROWS, :] = left_meas[pl.ds(first + half, LEFT_ROWS, stride=2), :]
        outs[distance][RIGHT_ROWS + LEFT_ROWS :, :] = meta


def assemble_kernel(place_ref, *refs):
    blocks, pieces, lefts = refs[:8], refs[8:10], refs[10:]
    for d in range(8):
        pieces[d // 4][(d % 4) * RIGHT_ROWS : (d % 4 + 1) * RIGHT_ROWS, :] = blocks[d][0:RIGHT_ROWS, :]
    for half in range(2):
        pieces[half][4 * RIGHT_ROWS :, :] = jnp.concatenate(
            [blocks[half * 4 + d][RIGHT_ROWS + LEFT_ROWS : RIGHT_ROWS + LEFT_ROWS + 2, :] for d in range(4)], axis=0
        )
    for dx in range(4):
        for dy in range(4):
            owner = ((place_ref[0] + dx) % 4) * 4 + (place_ref[1] + dy) % 4
            for d in range(8):
                row = (dy * 8 + d) * GQ
                lefts[dx][row : row + GQ, :] = blocks[d][pl.ds(RIGHT_ROWS + owner, GQ, stride=16), :]


CHUNK = 8


def final_kernel(*refs):
    lefts, pieces, total_ref = refs[:4], refs[4:36], refs[36]
    out_ref, rows, meta, factors, l_top, sem = refs[37:]
    step = pl.program_id(0) * pl.num_programs(1) + pl.program_id(1)

    @pl.when(step == 0)
    def _():
        copies = []
        for i, piece in enumerate(pieces):
            place, colour = i // 2, i % 2
            copies.append(
                pltpu.make_async_copy(
                    piece.at[pl.ds(0, 4 * RIGHT_ROWS)],
                    rows.at[pl.ds((place * 8 + colour * 4) * RIGHT_ROWS, 4 * RIGHT_ROWS)],
                    sem.at[0],
                )
            )
            copies.append(
                pltpu.make_async_copy(
                    piece.at[pl.ds(4 * RIGHT_ROWS, 8)],
                    meta.at[pl.ds((place * 2 + colour) * 8, 8)],
                    sem.at[0],
                )
            )
        for copy in copies:
            copy.start()
        for copy in copies:
            copy.wait()
        mine = meta[pl.ds(0, 128, stride=2), :]
        weight, key = mine[:, 0:1], mine[:, 1:2]
        diag = iota((128, 128), 0) == iota((128, 128), 1)
        key_row = jnp.sum(jnp.where(diag, key, 0.0), axis=0, keepdims=True)
        weight_row = jnp.sum(jnp.where(diag, weight, 0.0), axis=0, keepdims=True)
        own = jnp.sum(jnp.where(key == key_row, weight_row, 0.0), axis=1, keepdims=True)
        factors[...] = jnp.broadcast_to(weight / own, (128, 128))

    q = pl.program_id(0)

    @pl.when(pl.program_id(1) == 0)
    def _():
        left = jnp.concatenate([lefts[sy][pl.ds(q, 32, stride=GQ), :] for sy in range(4)], axis=0)
        hi, lo = split2(left * factors[...])
        l_top[...] = jnp.concatenate([hi, lo, hi], axis=0)

    left3 = l_top[...]
    for j in range(CHUNK):
        first = q * 32 + pl.program_id(1) * CHUNK + j
        hi, lo = split2(rows[pl.ds(first, 128, stride=RIGHT_ROWS), :])
        right3 = jnp.concatenate([hi, hi, lo], axis=0)
        cols = slice(j * 128, (j + 1) * 128)
        out_ref[0, :, cols] = total_ref[0, :, cols] + mm(left3, right3, TN)


ANY = pl.BlockSpec(memory_space=pl.ANY)
VMEM = pl.BlockSpec(memory_space=pltpu.VMEM)
SMEM = pl.BlockSpec(memory_space=pltpu.SMEM)


def sds(*shape):
    return jax.ShapeDtypeStruct(shape, F32)


def gather_plane(piece, first, second):
    up = [(i, (i + 1) % 4) for i in range(4)]
    down = [(i, (i - 1) % 4) for i in range(4)]
    line = {0: piece, 3: lax.ppermute(piece, first, up), 1: lax.ppermute(piece, first, down)}
    line[2] = lax.ppermute(line[3], first, up)
    found = {}
    for a in range(4):
        found[a, 0] = line[a]
        found[a, 3] = lax.ppermute(line[a], second, up)
        found[a, 1] = lax.ppermute(line[a], second, down)
        found[a, 2] = lax.ppermute(found[a, 3], second, up) if a % 2 == 0 else lax.ppermute(found[a, 1], second, down)
    return found if first == "x" else {(b, a): value for (a, b), value in found.items()}


def per_device(perturb, touched, spins, accept, site_ids, time_ids, left_proj, right_proj, weights, routing, total):
    column = lax.axis_index(("zh", "c", "zl"))
    group = lax.axis_index(("zh", "c"))
    chosen = touched.reshape(1, NS)
    gamma = (accept.astype(F32) * jnp.where(spins == 1, 0.6, -0.4).astype(F32)).reshape(1, NS)
    key = (routing[0] + 32 * group).astype(F32)
    blocks = pl.pallas_call(
        measure_kernel,
        out_shape=[sds(BLOCK_ROWS, 128)] * 8,
        in_specs=[SMEM] + [VMEM] * 6 + [SMEM, SMEM, ANY],
        out_specs=[VMEM] * 8,
        scratch_shapes=[
            pltpu.VMEM((K, K), F32),
            pltpu.VMEM((K, K), BF16),
            pltpu.VMEM((K, K), BF16),
            pltpu.VMEM((LEG, K), F32),
            pltpu.VMEM((LEG * Q, K), F32),
            pltpu.VMEM((2, Q, K), F32),
            pltpu.VMEM((Q * 32, 128), F32),
            pltpu.VMEM((Q * 32, 128), F32),
            pltpu.SemaphoreType.DMA,
        ],
        compiler_params=pltpu.CompilerParams(vmem_limit_bytes=56 * MIB),
        name="measure",
    )(column[None], chosen, gamma, site_ids, time_ids, left_proj, right_proj, weights, key, perturb)
    here = [blocks[0]] + [
        lax.ppermute(blocks[d], ("zh", "c", "zl"), [(i, i ^ d) for i in range(8)]) for d in range(1, 8)
    ]
    plane = jnp.stack([lax.axis_index("x"), lax.axis_index("y")]).astype(jnp.int32)
    first, second, *lefts = pl.pallas_call(
        assemble_kernel,
        out_shape=[sds(PIECE_ROWS, 128)] * 2 + [sds(128, 128)] * 4,
        in_specs=[SMEM] + [VMEM] * 8,
        out_specs=[VMEM] * 6,
        name="assemble",
    )(plane, *here)
    one, two = gather_plane(first, "x", "y"), gather_plane(second, "y", "x")
    from_x = {0: lefts[0]}
    for dx in range(1, 4):
        from_x[4 - dx] = lax.ppermute(lefts[dx], "x", [(i, (i + dx) % 4) for i in range(4)])
    rows_of = [jnp.concatenate([from_x[sx][dy * 32 : (dy + 1) * 32] for sx in range(4)], axis=0) for dy in range(4)]
    from_y = {0: rows_of[0]}
    for dy in range(1, 4):
        from_y[4 - dy] = lax.ppermute(rows_of[dy], "y", [(i, (i + dy) % 4) for i in range(4)])
    pieces = []
    for sy in range(4):
        for sx in range(4):
            pieces += [one[sx, sy], two[sx, sy]]
    block = pl.BlockSpec((1, 128, CHUNK * 128), lambda q, n: (q, 0, n))
    return pl.pallas_call(
        final_kernel,
        grid=(GQ, 32 // CHUNK),
        out_shape=sds(GQ, 128, SITES * LEG),
        in_specs=[VMEM] * 4 + [ANY] * 32 + [block],
        out_specs=block,
        scratch_shapes=[
            pltpu.VMEM((128 * RIGHT_ROWS, 128), F32),
            pltpu.VMEM((256, 128), F32),
            pltpu.VMEM((128, 128), F32),
            pltpu.VMEM((384, 128), BF16),
            pltpu.SemaphoreType.DMA((1,)),
        ],
        compiler_params=pltpu.CompilerParams(vmem_limit_bytes=40 * MIB),
        name="accumulate",
    )(*[from_y[sy] for sy in range(4)], *pieces, total)


def solution(mesh):
    cube = Mesh(mesh.devices.reshape(2, 2, 4, 4, 2), ("zh", "c", "x", "y", "zl"))
    grp, mem = ("zh", "c"), ("x", "y", "zl")
    both = grp + mem
    in_specs = (
        P(both, None, None),
        P(both, None, None),
        P(both, None, None),
        P(both, None, None),
        P(both, None),
        P(both, None),
        P(),
        P(),
        P(both),
        P(both, None),
        P(grp, mem, None),
    )
    return jax.shard_map(per_device, mesh=cube, in_specs=in_specs, out_specs=P(grp, mem, None), check_vma=False)
```

```python
import jax
import jax.numpy as jnp
import numpy as np
from jax import lax
from jax.experimental import pallas as pl
from jax.experimental.pallas import tpu as pltpu
from jax.sharding import Mesh
from jax.sharding import PartitionSpec as P


K = 1024
SITES = 64
LEG = 64
Q = 16
TIMES = 4096
UPDATES = 4
RANKB = 64
NS = UPDATES * RANKB
GQ = 4
RIGHT_ROWS = GQ * 32
LEFT_ROWS = GQ * 16
BLOCK_ROWS = RIGHT_ROWS + LEFT_ROWS + 8
F32 = jnp.float32
BF16 = jnp.bfloat16
NN = (((1,), (0,)), ((), ()))
NT = (((1,), (1,)), ((), ()))
TN = (((0,), (0,)), ((), ()))
MIB = 1 << 20


def mm(a, b, dims=NN):
    return lax.dot_general(a, b, dims, preferred_element_type=F32)


def split2(x):
    hi = x.astype(BF16)
    return hi, (x - hi.astype(F32)).astype(BF16)


def split3(x):
    hi = x.astype(BF16)
    rest = x - hi.astype(F32)
    mid = rest.astype(BF16)
    return hi, mid, (rest - mid.astype(F32)).astype(BF16)


def mm3(a, b, dims=NN):
    ah, al = a if isinstance(a, tuple) else split2(a)
    bh, bl = b if isinstance(b, tuple) else split2(b)
    rows = ah.shape[0]
    top = mm(jnp.concatenate([ah, al], axis=0), bh, dims)
    return top[:rows] + (top[rows:] + mm(ah, bl, dims))


def iota(shape, dim):
    return lax.broadcasted_iota(jnp.int32, shape, dim)


def row_to_column(row):
    n = row.shape[1]
    same = iota((n, n), 0) == iota((n, n), 1)
    return jnp.sum(jnp.where(same, row, jnp.zeros_like(row)), axis=1, keepdims=True)


def measure_kernel(
    chosen_ref, spin_ref, accept_ref, site_ref, time_ref, left_ref, right_ref, weight_ref, routing_ref, perturb_ref,
    *rest,
):
    outs = rest[:8]
    (matrix, p_hi, p_lo, polys, spread, vecs, left_meas, right_meas, sem) = rest[8:]
    load = pltpu.make_async_copy(perturb_ref.at[0], matrix, sem)
    load.start()

    abscissa = (2.0 * time_ref[...].astype(F32) + 1.0) / TIMES - 1.0
    before, now = jnp.ones_like(abscissa), abscissa
    polys[0:1, :] = before
    polys[1:2, :] = now * float(np.sqrt(3.0))
    for degree in range(1, LEG - 1):
        after = abscissa * now * ((2 * degree + 1) / (degree + 1)) - before * (degree / (degree + 1))
        before, now = now, after
        polys[degree + 1 : degree + 2, :] = now * float(np.sqrt(2.0 * degree + 3.0))

    sites = site_ref[...]
    onehot = (iota((SITES, K), 0) == sites).astype(F32).astype(BF16)
    onehot3 = jnp.concatenate([onehot, onehot, onehot], axis=0)
    for side, table_ref in ((0, left_ref), (1, right_ref)):
        table = jnp.concatenate(split3(table_ref[...]), axis=0)
        spread[...] = mm(table, onehot3, TN)
        total = jnp.zeros((Q, K), F32)
        for degree in range(LEG):
            total = total + spread[degree * Q : (degree + 1) * Q, :] * polys[degree : degree + 1, :]
        vecs[side] = total

    def one_row(values):
        return jnp.concatenate([values[u : u + 1, :] for u in range(UPDATES)], axis=1)

    chosen = row_to_column(one_row(chosen_ref[0].astype(F32))).astype(jnp.int32)
    pick = (iota((NS, K), 1) == chosen).astype(F32).astype(BF16)
    gamma = one_row(accept_ref[0].astype(F32) * jnp.where(spin_ref[0] == 1, 0.6, -0.4))
    gamma_column = row_to_column(gamma)
    load.wait()
    for step in range(4):
        rows = slice(step * 256, (step + 1) * 256)
        hi, lo = split2(matrix[rows, :])
        p_hi[rows, :] = hi
        p_lo[rows, :] = lo
    ph, plo = p_hi[...], p_lo[...]
    v, w = vecs[0], vecs[1]
    wh, wl = split2(w)
    high = mm(jnp.concatenate([pick, wh, wl], axis=0), ph)
    low = mm(jnp.concatenate([pick, wh], axis=0), plo)
    rows_hi, rows_lo = high[:NS].astype(BF16), low[:NS].astype(BF16)
    from_w = high[NS : NS + Q] + high[NS + Q :] + low[NS:]
    same = mm(pick, pick, NT)
    small = mm(rows_hi, pick, NT) + mm(rows_lo, pick, NT)
    vs = split3(v)
    p_vec = mm(pick, vs[0], NT) + mm(pick, vs[1], NT) + mm(pick, vs[2], NT)
    p_vec = p_vec + mm3((rows_hi, rows_lo), (vs[0], vs[1]), NT)
    fs = split3(from_w)
    q_vec = mm(fs[0], pick, NT) + mm(fs[1], pick, NT) + mm(fs[2], pick, NT)
    row_block = lax.div(iota((NS, NS), 0), RANKB)
    col_block = lax.div(iota((NS, NS), 1), RANKB)
    c_all, r_all = jnp.zeros((NS, NS), F32), jnp.zeros((NS, NS), F32)
    x, y = jnp.zeros((NS, Q), F32), jnp.zeros((Q, NS), F32)
    for update in range(UPDATES):
        mine = col_block == update
        columns = jnp.where(mine, small * gamma, 0.0)
        y_now = jnp.where(mine[:Q], q_vec * gamma, 0.0)
        rows_now = small + same
        x = jnp.where(row_block[:, :Q] == update, p_vec, x)
        y = y + y_now
        if update < UPDATES - 1:
            c_all = c_all + columns
            r_all = jnp.where(row_block == update, rows_now, r_all)
            change = mm3(jnp.concatenate([columns, y_now], axis=0), rows_now)
            p_vec = p_vec - mm3(columns, p_vec)
            small = small - change[:NS]
            q_vec = q_vec - change[NS:]
    lower = split2(jnp.where(row_block > col_block, c_all, 0.0))
    upper = split2(jnp.where(row_block < col_block, r_all, 0.0) * gamma)
    lower_twice, upper_twice = split2(mm3(lower, lower)), split2(mm3(upper, upper))
    z = x + mm3(upper_twice, x)
    y2 = y + mm3(y, lower_twice)
    z = z - mm3(upper, z)
    y2 = y2 - mm3(y2, lower)
    zs, ys = split3(z * gamma_column), split3(y2)
    left_arg = v - (mm(zs[0], pick, TN) + mm(zs[1], pick, TN) + mm(zs[2], pick, TN))
    left_image = v + mm3(left_arg, (ph, plo), NT)
    right_arg = w - (mm(ys[0], pick) + mm(ys[1], pick) + mm(ys[2], pick))
    right_image = right_arg + from_w - mm3((ys[0], ys[1]), (rows_hi, rows_lo))

    odd = lax.rem(sites, 2).astype(F32)
    values = polys[...]
    values = jnp.concatenate([values * (1.0 - odd), values * odd], axis=0)
    both = jnp.concatenate(split2(values), axis=0)
    pair = iota((32, K), 0) == lax.div(sites, 2)
    for image, meas in ((right_image, right_meas), (left_image, left_meas)):
        ih = image.astype(BF16).astype(F32)
        il = image - ih

        def masked(part):
            return jnp.concatenate(
                [jnp.where(pair, part[q : q + 1, :], 0.0).astype(BF16) for q in range(Q)], axis=0
            )

        high = mm(masked(ih), both, NT)
        low = mm(masked(il), both[:128], NT)
        meas[...] = high[:, :128] + (high[:, 128:] + low)

    lane = iota((8, 128), 1)
    own_group = lax.axis_index("zh") * 2 + lax.axis_index("c")
    key = (routing_ref[0, 0] + 32 * own_group).astype(F32)
    meta = jnp.where(lane == 0, weight_ref[0], jnp.where(lane == 1, key, 0.0))
    for distance in range(8):
        target = (own_group * 2 + lax.axis_index("zl")) ^ distance
        group, half = target // 2, target % 2
        first = pl.multiple_of(group * RIGHT_ROWS, RIGHT_ROWS)
        outs[distance][0:RIGHT_ROWS, :] = right_meas[pl.ds(first, RIGHT_ROWS), :]
        outs[distance][RIGHT_ROWS : RIGHT_ROWS + LEFT_ROWS, :] = left_meas[pl.ds(first + half, LEFT_ROWS, stride=2), :]
        outs[distance][RIGHT_ROWS + LEFT_ROWS :, :] = meta


TILE_META = 64
HALF = 32


def assemble_kernel(*refs):
    blocks, outs = refs[:8], (refs[8:11], refs[11:14])
    place = (lax.axis_index("x"), lax.axis_index("y"))
    for colour in range(2):
        up, down, own = outs[colour]
        size = 65 - colour
        for d in range(8):
            rows = blocks[d][colour * 64 : (colour + 1) * 64, :]
            up[0:64, d, :] = rows
            down[0:64, d, :] = rows
            if colour == 0:
                first = RIGHT_ROWS + LEFT_ROWS
                up[TILE_META, d : d + 1, :] = blocks[d][first : first + 1, :]
                down[TILE_META, d : d + 1, :] = blocks[d][first : first + 1, :]

        def fill(ref, at, along, across):
            shift = (along, across) if colour == 0 else (across, along)
            owner = ((place[0] + shift[0]) % 4) * 4 + (place[1] + shift[1]) % 4
            for d in range(8):
                rows = blocks[d][pl.ds(RIGHT_ROWS + colour * 32 + owner, 2, stride=16), :]
                ref[at, d : d + 1, :] = rows[0:1]
                ref[at + 1, d : d + 1, :] = rows[1:2]

        for across in range(4):
            fill(up, size + 2 * across, 1, across)
            fill(down, size + 2 * across, 3, across)
            fill(own, 2 * across, 0, across)
        for k in range(2):
            fill(up, size + 8 + 2 * k, 2, k)
            fill(down, size + 8 + 2 * k, 2, 2 + k)


CHUNK = 8
STEPS = 32 // CHUNK


def find_tiles(colour):
    n = 65 - colour
    P, OWN, A, B, C, D, E, F, G, H, I, J = range(12)
    right = {
        (0, 0): ((P, 0), (P, HALF)),
        (3, 0): ((A, 0), (A, HALF)),
        (1, 0): ((B, 0), (B, HALF)),
        (2, 0): ((C, 0), (D, 0)),
        (0, 2): ((I, 0), (I, HALF)),
        (3, 2): ((I, n), (J, 0)),
        (1, 2): ((J, n - HALF), (J, n)),
        (2, 2): ((I, n + HALF), (J, 2 * n - HALF)),
    }
    left = {
        (0, 0): (OWN, 0),
        (3, 0): (A, n),
        (1, 0): (B, n),
        (2, 0): (C, HALF),
        (0, 2): (I, n + 2 * HALF),
        (3, 2): (I, n + 2 * HALF + 2),
        (1, 2): (J, 3 * n - 2 * HALF),
        (2, 2): (J, 3 * n - 2 * HALF + 2),
    }
    for across, near, far in ((3, E, G), (1, F, H)):
        for i, along in enumerate((0, 3, 1)):
            right[along, across] = ((near, i * n), (near, i * n + HALF))
        right[2, across] = ((far, 0), (far, HALF))
        for i, along in enumerate((0, 3, 1, 2)):
            left[along, across] = (far, n + 2 * i)
    order = [(sx, sy) for sy in range(4) for sx in range(4)]
    if colour == 1:
        order = [(sy, sx) for sx, sy in order]
    return [right[place] for place in order], [left[place] for place in order]


def final_kernel(*refs):
    buffers, total_ref, out_ref, l_top, totals, results, sem = (refs[:12], refs[12:24]), *refs[24:]
    tiles = [find_tiles(colour) for colour in range(2)]

    def columns_of(step):
        n = lax.rem(step, STEPS)
        return lax.div(step, STEPS), pl.ds(pl.multiple_of(n * CHUNK * 128, CHUNK * 128), CHUNK * 128)

    def fetch(step):
        q, cols = columns_of(step)
        slot = lax.rem(step, 2)
        return pltpu.make_async_copy(total_ref.at[q, :, cols], totals.at[slot], sem.at[slot])

    def store(step):
        q, cols = columns_of(step)
        slot = lax.rem(step, 2)
        return pltpu.make_async_copy(results.at[slot], out_ref.at[q, :, cols], sem.at[2 + slot])

    for step in range(2):
        fetch(step).start()
    metas = []
    for halves in tiles[0][0]:
        which, first = halves[1]
        metas.append(buffers[0][which][first + TILE_META - HALF])
    mine = jnp.concatenate(metas, axis=0)
    weight, key = mine[:, 0:1], mine[:, 1:2]
    diag = iota((128, 128), 0) == iota((128, 128), 1)
    key_row = jnp.sum(jnp.where(diag, key, 0.0), axis=0, keepdims=True)
    weight_row = jnp.sum(jnp.where(diag, weight, 0.0), axis=0, keepdims=True)
    own = jnp.sum(jnp.where(key == key_row, weight_row, 0.0), axis=1, keepdims=True)
    factors = weight / own
    for q in range(GQ):
        colour, k = q // 2, q % 2
        left = jnp.concatenate([buffers[colour][which][first + k] for which, first in tiles[colour][1]], axis=0)
        hi, lo = split2((left * factors).T)
        l_top[q] = jnp.concatenate([hi, lo, hi], axis=1)

    for q in range(GQ):
        places = [halves[q % 2] for halves in tiles[q // 2][0]]

        def body(n, carry):
            step = q * STEPS + n
            slot = lax.rem(step, 2)
            fetch(step).wait()

            @pl.when(step >= 2)
            def _():
                store(step).wait()

            left3 = l_top[q]
            for j in range(0, CHUNK, 2):
                right = jnp.concatenate(
                    [
                        jnp.concatenate(
                            [buffers[q // 2][which][first + n * CHUNK + j + k] for which, first in places], axis=0
                        )
                        for k in range(2)
                    ],
                    axis=1,
                )
                hi, lo = split2(right)
                right3 = jnp.concatenate([hi, hi, lo], axis=0)
                cols = slice(j * 128, (j + 2) * 128)
                results[slot, :, cols] = totals[slot, :, cols] + mm(left3, right3)
            store(step).start()

            @pl.when(step + 2 < GQ * STEPS)
            def _():
                fetch(step + 2).start()

            return carry

        lax.fori_loop(0, STEPS, body, 0)
    for slot in range(2):
        store(slot).wait()


ANY = pl.BlockSpec(memory_space=pl.ANY)
VMEM = pl.BlockSpec(memory_space=pltpu.VMEM)
SMEM = pl.BlockSpec(memory_space=pltpu.SMEM)


def sds(*shape):
    return jax.ShapeDtypeStruct(shape, F32)


UP = [(i, (i + 1) % 4) for i in range(4)]
DOWN = [(i, (i - 1) % 4) for i in range(4)]


def hop(axis, way, value):
    return lax.ppermute(value, axis, way)


def gather_planes(colours):
    axes = (("x", "y"), ("y", "x"))
    state = []
    for (first, _), (up, down, own) in zip(axes, colours):
        state.append([up, own, hop(first, UP, up), hop(first, DOWN, down)])
    for (first, _), found, size in zip(axes, state, (65, 64)):
        a, b = found[2], found[3]
        found.append(hop(first, UP, jnp.concatenate([a[:HALF], a[size + 8 :]], axis=0)))
        found.append(hop(first, DOWN, jnp.concatenate([b[HALF:size], b[size + 8 :]], axis=0)))
    for (_, second), found, size in zip(axes, state, (65, 64)):
        line = jnp.concatenate([found[0][:size], found[2][:size], found[3][:size]], axis=0)
        found.append(hop(second, UP, line))
        found.append(hop(second, DOWN, line))
    for (_, second), found, size in zip(axes, state, (65, 64)):
        _, own, a, b, c, d = found[:6]
        n = size
        opposite = [c[:HALF], d[: n - HALF]]
        up = [own[2:4], a[n + 2 : n + 4], b[n + 2 : n + 4], c[HALF + 2 : HALF + 4], own[4:6], a[n + 4 : n + 6]]
        down = [own[6:8], a[n + 6 : n + 8], b[n + 6 : n + 8], d[n - HALF + 2 :], b[n + 4 : n + 6], d[n - HALF : n - HALF + 2]]
        found.append(hop(second, UP, jnp.concatenate(opposite + up, axis=0)))
        found.append(hop(second, DOWN, jnp.concatenate(opposite + down, axis=0)))
    for (_, second), found, n in zip(axes, state, (65, 64)):
        e, f, g, h = found[6:10]
        cut = n + HALF
        found.append(hop(second, UP, jnp.concatenate([e[:cut], g[:HALF], g[n + 8 :]], axis=0)))
        found.append(hop(second, DOWN, jnp.concatenate([f[cut:], h[HALF:n], h[n + 8 :]], axis=0)))
    return state


def per_device(perturb, touched, spins, accept, site_ids, time_ids, left_proj, right_proj, weights, routing, total):
    blocks = pl.pallas_call(
        measure_kernel,
        out_shape=[sds(BLOCK_ROWS, 128)] * 8,
        in_specs=[VMEM] * 7 + [SMEM, SMEM, ANY],
        out_specs=[VMEM] * 8,
        scratch_shapes=[
            pltpu.VMEM((K, K), F32),
            pltpu.VMEM((K, K), BF16),
            pltpu.VMEM((K, K), BF16),
            pltpu.VMEM((LEG, K), F32),
            pltpu.VMEM((LEG * Q, K), F32),
            pltpu.VMEM((2, Q, K), F32),
            pltpu.VMEM((Q * 32, 128), F32),
            pltpu.VMEM((Q * 32, 128), F32),
            pltpu.SemaphoreType.DMA,
        ],
        compiler_params=pltpu.CompilerParams(vmem_limit_bytes=56 * MIB),
        name="measure",
    )(touched, spins, accept, site_ids, time_ids, left_proj, right_proj, weights, routing, perturb)
    here = [blocks[0]] + [
        lax.ppermute(blocks[d], ("zh", "c", "zl"), [(i, i ^ d) for i in range(8)]) for d in range(1, 8)
    ]
    packed = pl.pallas_call(
        assemble_kernel,
        out_shape=[sds(77, 8, 128), sds(77, 8, 128), sds(8, 8, 128), sds(76, 8, 128), sds(76, 8, 128), sds(8, 8, 128)],
        in_specs=[VMEM] * 8,
        out_specs=[VMEM] * 6,
        name="assemble",
    )(*here)
    one, two = gather_planes((packed[:3], packed[3:]))
    return pl.pallas_call(
        final_kernel,
        out_shape=sds(GQ, 128, SITES * LEG),
        in_specs=[VMEM] * 24 + [ANY],
        out_specs=ANY,
        scratch_shapes=[
            pltpu.VMEM((GQ, 128, 384), BF16),
            pltpu.VMEM((2, 128, CHUNK * 128), F32),
            pltpu.VMEM((2, 128, CHUNK * 128), F32),
            pltpu.SemaphoreType.DMA((4,)),
        ],
        compiler_params=pltpu.CompilerParams(vmem_limit_bytes=30 * MIB),
        name="accumulate",
    )(*one, *two, total)


def solution(mesh):
    cube = Mesh(mesh.devices.reshape(2, 2, 4, 4, 2), ("zh", "c", "x", "y", "zl"))
    grp, mem = ("zh", "c"), ("x", "y", "zl")
    both = grp + mem
    in_specs = (
        P(both, None, None),
        P(both, None, None),
        P(both, None, None),
        P(both, None, None),
        P(both, None),
        P(both, None),
        P(),
        P(),
        P(both),
        P(both, None),
        P(grp, mem, None),
    )
    return jax.shard_map(per_device, mesh=cube, in_specs=in_specs, out_specs=P(grp, mem, None), check_vma=False)
```

```python
import jax
import jax.numpy as jnp
import numpy as np
from jax import lax
from jax.experimental import pallas as pl
from jax.experimental.pallas import tpu as pltpu
from jax.sharding import Mesh
from jax.sharding import PartitionSpec as P


K = 1024
SITES = 64
LEG = 64
Q = 16
TIMES = 4096
UPDATES = 4
RANKB = 64
NS = UPDATES * RANKB
GQ = 4
RIGHT_ROWS = GQ * 32
LEFT_ROWS = GQ * 16
BLOCK_ROWS = RIGHT_ROWS + LEFT_ROWS + 8
F32 = jnp.float32
BF16 = jnp.bfloat16
NN = (((1,), (0,)), ((), ()))
NT = (((1,), (1,)), ((), ()))
TN = (((0,), (0,)), ((), ()))
MIB = 1 << 20


def mm(a, b, dims=NN):
    return lax.dot_general(a, b, dims, preferred_element_type=F32)


def split2(x):
    hi = x.astype(BF16)
    return hi, (x - hi.astype(F32)).astype(BF16)


def split3(x):
    hi = x.astype(BF16)
    rest = x - hi.astype(F32)
    mid = rest.astype(BF16)
    return hi, mid, (rest - mid.astype(F32)).astype(BF16)


def mm3(a, b, dims=NN):
    ah, al = a if isinstance(a, tuple) else split2(a)
    bh, bl = b if isinstance(b, tuple) else split2(b)
    rows = ah.shape[0]
    top = mm(jnp.concatenate([ah, al], axis=0), bh, dims)
    return top[:rows] + (top[rows:] + mm(ah, bl, dims))


def iota(shape, dim):
    return lax.broadcasted_iota(jnp.int32, shape, dim)


def row_to_column(row):
    n = row.shape[1]
    same = iota((n, n), 0) == iota((n, n), 1)
    return jnp.sum(jnp.where(same, row, jnp.zeros_like(row)), axis=1, keepdims=True)


def measure_kernel(
    chosen_ref, spin_ref, accept_ref, site_ref, time_ref, left_ref, right_ref, weight_ref, routing_ref, perturb_ref,
    *rest,
):
    outs = rest[:8]
    (matrix, p_hi, p_lo, polys, spread, vecs, left_meas, right_meas, sem) = rest[8:]
    load = pltpu.make_async_copy(perturb_ref.at[0], matrix, sem)
    load.start()

    abscissa = (2.0 * time_ref[...].astype(F32) + 1.0) / TIMES - 1.0
    before, now = jnp.ones_like(abscissa), abscissa
    polys[0:1, :] = before
    polys[1:2, :] = now * float(np.sqrt(3.0))
    for degree in range(1, LEG - 1):
        after = abscissa * now * ((2 * degree + 1) / (degree + 1)) - before * (degree / (degree + 1))
        before, now = now, after
        polys[degree + 1 : degree + 2, :] = now * float(np.sqrt(2.0 * degree + 3.0))

    sites = site_ref[...]
    onehot = (iota((SITES, K), 0) == sites).astype(F32).astype(BF16)
    onehot3 = jnp.concatenate([onehot, onehot, onehot], axis=0)
    for side, table_ref in ((0, left_ref), (1, right_ref)):
        table = jnp.concatenate(split3(table_ref[...]), axis=0)
        spread[...] = mm(table, onehot3, TN)
        total = jnp.zeros((Q, K), F32)
        for degree in range(LEG):
            total = total + spread[degree * Q : (degree + 1) * Q, :] * polys[degree : degree + 1, :]
        vecs[side] = total

    def one_row(values):
        return jnp.concatenate([values[u : u + 1, :] for u in range(UPDATES)], axis=1)

    chosen = row_to_column(one_row(chosen_ref[0].astype(F32))).astype(jnp.int32)
    pick = (iota((NS, K), 1) == chosen).astype(F32).astype(BF16)
    gamma = one_row(accept_ref[0].astype(F32) * jnp.where(spin_ref[0] == 1, 0.6, -0.4))
    gamma_column = row_to_column(gamma)
    load.wait()
    for step in range(4):
        rows = slice(step * 256, (step + 1) * 256)
        hi, lo = split2(matrix[rows, :])
        p_hi[rows, :] = hi
        p_lo[rows, :] = lo
    ph, plo = p_hi[...], p_lo[...]
    v, w = vecs[0], vecs[1]
    wh, wl = split2(w)
    high = mm(jnp.concatenate([pick, wh, wl], axis=0), ph)
    low = mm(jnp.concatenate([pick, wh], axis=0), plo)
    rows_hi, rows_lo = high[:NS].astype(BF16), low[:NS].astype(BF16)
    from_w = high[NS : NS + Q] + high[NS + Q :] + low[NS:]
    same = mm(pick, pick, NT)
    small = mm(rows_hi, pick, NT) + mm(rows_lo, pick, NT)
    vs = split3(v)
    p_vec = mm(pick, vs[0], NT) + mm(pick, vs[1], NT) + mm(pick, vs[2], NT)
    p_vec = p_vec + mm3((rows_hi, rows_lo), (vs[0], vs[1]), NT)
    fs = split3(from_w)
    q_vec = mm(fs[0], pick, NT) + mm(fs[1], pick, NT) + mm(fs[2], pick, NT)
    row_block = lax.div(iota((NS, NS), 0), RANKB)
    col_block = lax.div(iota((NS, NS), 1), RANKB)
    c_all, r_all = jnp.zeros((NS, NS), F32), jnp.zeros((NS, NS), F32)
    x, y = jnp.zeros((NS, Q), F32), jnp.zeros((Q, NS), F32)
    for update in range(UPDATES):
        mine = col_block == update
        columns = jnp.where(mine, small * gamma, 0.0)
        y_now = jnp.where(mine[:Q], q_vec * gamma, 0.0)
        rows_now = small + same
        x = jnp.where(row_block[:, :Q] == update, p_vec, x)
        y = y + y_now
        if update < UPDATES - 1:
            c_all = c_all + columns
            r_all = jnp.where(row_block == update, rows_now, r_all)
            half = slice(update // 2 * 128, update // 2 * 128 + 128)
            columns, y_now, rows_now = columns[:, half], y_now[:, half], split2(rows_now[half])
            change = mm3(jnp.concatenate([columns, y_now], axis=0), rows_now)
            p_vec = p_vec - mm3(columns, p_vec[half])
            small = small - change[:NS]
            q_vec = q_vec - change[NS:]
    lower = split2(jnp.where(row_block > col_block, c_all, 0.0))
    upper = split2(jnp.where(row_block < col_block, r_all, 0.0) * gamma)
    lower_twice, upper_twice = split2(mm3(lower, lower)), split2(mm3(upper, upper))
    z = x + mm3(upper_twice, x)
    y2 = y + mm3(y, lower_twice)
    z = z - mm3(upper, z)
    y2 = y2 - mm3(y2, lower)
    zs, ys = split3(z * gamma_column), split3(y2)
    left_arg = v - (mm(zs[0], pick, TN) + mm(zs[1], pick, TN) + mm(zs[2], pick, TN))
    ah, al = split2(left_arg)
    streamed = mm(ph, jnp.concatenate([ah, al], axis=0), NT)
    streamed = streamed[:, :Q] + (streamed[:, Q:] + mm(plo, ah, NT))
    left_image = v + streamed.T
    right_arg = w - (mm(ys[0], pick) + mm(ys[1], pick) + mm(ys[2], pick))
    right_image = right_arg + from_w - mm3((ys[0], ys[1]), (rows_hi, rows_lo))

    odd = lax.rem(sites, 2).astype(F32)
    values = polys[...]
    values = jnp.concatenate([values * (1.0 - odd), values * odd], axis=0)
    both = jnp.concatenate(split2(values), axis=0)
    pair = iota((32, K), 0) == lax.div(sites, 2)
    for image, meas in ((right_image, right_meas), (left_image, left_meas)):
        ih = image.astype(BF16).astype(F32)
        il = image - ih

        def masked(part):
            return jnp.concatenate(
                [jnp.where(pair, part[q : q + 1, :], 0.0).astype(BF16) for q in range(Q)], axis=0
            )

        high = mm(masked(ih), both, NT)
        low = mm(masked(il), both[:128], NT)
        meas[...] = high[:, :128] + (high[:, 128:] + low)

    lane = iota((8, 128), 1)
    own_group = lax.axis_index("zh") * 2 + lax.axis_index("c")
    key = (routing_ref[0, 0] + 32 * own_group).astype(F32)
    meta = jnp.where(lane == 0, weight_ref[0], jnp.where(lane == 1, key, 0.0))
    for distance in range(8):
        target = (own_group * 2 + lax.axis_index("zl")) ^ distance
        group, half = target // 2, target % 2
        first = pl.multiple_of(group * RIGHT_ROWS, RIGHT_ROWS)
        outs[distance][0:RIGHT_ROWS, :] = right_meas[pl.ds(first, RIGHT_ROWS), :]
        outs[distance][RIGHT_ROWS : RIGHT_ROWS + LEFT_ROWS, :] = left_meas[pl.ds(first + half, LEFT_ROWS, stride=2), :]
        outs[distance][RIGHT_ROWS + LEFT_ROWS :, :] = meta


TILE_META = 64
HALF = 32


def assemble_kernel(*refs):
    blocks, outs = refs[:8], (refs[8:11], refs[11:14])
    place = (lax.axis_index("x"), lax.axis_index("y"))
    for colour in range(2):
        up, down, own = outs[colour]
        size = 65 - colour
        for d in range(8):
            rows = blocks[d][colour * 64 : (colour + 1) * 64, :]
            for ref in (up, down):
                ref[pl.ds(d, 64, stride=8), :] = rows
                if colour == 0:
                    first = RIGHT_ROWS + LEFT_ROWS
                    ref[TILE_META * 8 + d : TILE_META * 8 + d + 1, :] = blocks[d][first : first + 1, :]

        def fill(ref, at, along, across):
            shift = (along, across) if colour == 0 else (across, along)
            owner = ((place[0] + shift[0]) % 4) * 4 + (place[1] + shift[1]) % 4
            for d in range(8):
                rows = blocks[d][pl.ds(RIGHT_ROWS + colour * 32 + owner, 2, stride=16), :]
                ref[pl.ds(at * 8 + d, 2, stride=8), :] = rows

        for across in range(4):
            fill(up, size + 2 * across, 1, across)
            fill(down, size + 2 * across, 3, across)
            fill(own, 2 * across, 0, across)
        for k in range(2):
            fill(up, size + 8 + 2 * k, 2, k)
            fill(down, size + 8 + 2 * k, 2, 2 + k)


CHUNK = 8
STEPS = 32 // CHUNK


def find_tiles(colour):
    n = 65 - colour
    P, OWN, A, B, C, D, E, F, G, H, I, J = range(12)
    right = {
        (0, 0): ((P, 0), (P, HALF)),
        (3, 0): ((A, 0), (A, HALF)),
        (1, 0): ((B, 0), (B, HALF)),
        (2, 0): ((C, 0), (D, 0)),
        (0, 2): ((I, 0), (I, HALF)),
        (3, 2): ((I, n), (J, 0)),
        (1, 2): ((J, n - HALF), (J, n)),
        (2, 2): ((I, n + HALF), (J, 2 * n - HALF)),
    }
    left = {
        (0, 0): (OWN, 0),
        (3, 0): (A, n),
        (1, 0): (B, n),
        (2, 0): (C, HALF),
        (0, 2): (I, n + 2 * HALF),
        (3, 2): (I, n + 2 * HALF + 2),
        (1, 2): (J, 3 * n - 2 * HALF),
        (2, 2): (J, 3 * n - 2 * HALF + 2),
    }
    for across, near, far in ((3, E, G), (1, F, H)):
        for i, along in enumerate((0, 3, 1)):
            right[along, across] = ((near, i * n), (near, i * n + HALF))
        right[2, across] = ((far, 0), (far, HALF))
        for i, along in enumerate((0, 3, 1, 2)):
            left[along, across] = (far, n + 2 * i)
    order = [(sx, sy) for sy in range(4) for sx in range(4)]
    if colour == 1:
        order = [(sy, sx) for sx, sy in order]
    return [right[place] for place in order], [left[place] for place in order]


def final_kernel(*refs):
    buffers, total_ref, out_ref, l_top, totals, results, sem = (refs[:12], refs[12:24]), *refs[24:]
    tiles = [find_tiles(colour) for colour in range(2)]

    def columns_of(step):
        n = lax.rem(step, STEPS)
        return lax.div(step, STEPS), pl.ds(pl.multiple_of(n * CHUNK * 128, CHUNK * 128), CHUNK * 128)

    def fetch(step):
        q, cols = columns_of(step)
        slot = lax.rem(step, 2)
        return pltpu.make_async_copy(total_ref.at[q, :, cols], totals.at[slot], sem.at[slot])

    def store(step):
        q, cols = columns_of(step)
        slot = lax.rem(step, 2)
        return pltpu.make_async_copy(results.at[slot], out_ref.at[q, :, cols], sem.at[2 + slot])

    for step in range(2):
        fetch(step).start()
    metas = []
    for halves in tiles[0][0]:
        which, first = halves[1]
        metas.append(buffers[0][which][first + TILE_META - HALF])
    mine = jnp.concatenate(metas, axis=0)
    weight, key = mine[:, 0:1], mine[:, 1:2]
    diag = iota((128, 128), 0) == iota((128, 128), 1)
    key_row = jnp.sum(jnp.where(diag, key, 0.0), axis=0, keepdims=True)
    weight_row = jnp.sum(jnp.where(diag, weight, 0.0), axis=0, keepdims=True)
    own = jnp.sum(jnp.where(key == key_row, weight_row, 0.0), axis=1, keepdims=True)
    factors = weight / own
    for q in range(GQ):
        colour, k = q // 2, q % 2
        left = jnp.concatenate([buffers[colour][which][first + k] for which, first in tiles[colour][1]], axis=0)
        hi, lo = split2((left * factors).T)
        l_top[q] = jnp.concatenate([hi, lo, hi], axis=1)

    for q in range(GQ):
        places = [halves[q % 2] for halves in tiles[q // 2][0]]

        def body(n, carry):
            step = q * STEPS + n
            slot = lax.rem(step, 2)
            fetch(step).wait()

            @pl.when(step >= 2)
            def _():
                store(step).wait()

            left3 = l_top[q]
            for j in range(0, CHUNK, 2):
                right = jnp.concatenate(
                    [
                        jnp.concatenate(
                            [buffers[q // 2][which][first + n * CHUNK + j + k] for which, first in places], axis=0
                        )
                        for k in range(2)
                    ],
                    axis=1,
                )
                hi, lo = split2(right)
                right3 = jnp.concatenate([hi, hi, lo], axis=0)
                cols = slice(j * 128, (j + 2) * 128)
                results[slot, :, cols] = totals[slot, :, cols] + mm(left3, right3)
            store(step).start()

            @pl.when(step + 2 < GQ * STEPS)
            def _():
                fetch(step + 2).start()

            return carry

        lax.fori_loop(0, STEPS, body, 0)
    for slot in range(2):
        store(slot).wait()


ANY = pl.BlockSpec(memory_space=pl.ANY)
VMEM = pl.BlockSpec(memory_space=pltpu.VMEM)
SMEM = pl.BlockSpec(memory_space=pltpu.SMEM)


def sds(*shape):
    return jax.ShapeDtypeStruct(shape, F32)


UP = [(i, (i + 1) % 4) for i in range(4)]
DOWN = [(i, (i - 1) % 4) for i in range(4)]


FAR_FIRST = (4, 6, 5, 7, 1, 3, 2)


def hop(axis, way, *parts):
    value = jnp.concatenate(parts, axis=0) if len(parts) > 1 else parts[0]
    return lax.ppermute(value, axis, way)


def gather_planes(colours):
    axes = (("x", "y"), ("y", "x"))
    state = []
    for (first, _), (up, down, own) in zip(axes, colours):
        state.append([up, own, hop(first, UP, up), hop(first, DOWN, down)])
    for (first, _), found, size in zip(axes, state, (65, 64)):
        a, b = found[2], found[3]
        found.append(hop(first, UP, a[:HALF], a[size + 8 :]))
        found.append(hop(first, DOWN, b[HALF:size], b[size + 8 :]))
    for (_, second), found, size in zip(axes, state, (65, 64)):
        line = jnp.concatenate([found[0][:size], found[2][:size], found[3][:size]], axis=0)
        found.append(hop(second, UP, line))
        found.append(hop(second, DOWN, line))
    for (_, second), found, size in zip(axes, state, (65, 64)):
        _, own, a, b, c, d = found[:6]
        n = size
        opposite = [c[:HALF], d[: n - HALF]]
        up = [own[2:4], a[n + 2 : n + 4], b[n + 2 : n + 4], c[HALF + 2 : HALF + 4], own[4:6], a[n + 4 : n + 6]]
        down = [own[6:8], a[n + 6 : n + 8], b[n + 6 : n + 8], d[n - HALF + 2 :], b[n + 4 : n + 6], d[n - HALF : n - HALF + 2]]
        found.append(hop(second, UP, *opposite, *up))
        found.append(hop(second, DOWN, *opposite, *down))
    for (_, second), found, n in zip(axes, state, (65, 64)):
        e, f, g, h = found[6:10]
        cut = n + HALF
        found.append(hop(second, UP, e[:cut], g[:HALF], g[n + 8 :]))
        found.append(hop(second, DOWN, f[cut:], h[HALF:n], h[n + 8 :]))
    return state


def per_device(perturb, touched, spins, accept, site_ids, time_ids, left_proj, right_proj, weights, routing, total):
    blocks = pl.pallas_call(
        measure_kernel,
        out_shape=[sds(BLOCK_ROWS, 128)] * 8,
        in_specs=[VMEM] * 7 + [SMEM, SMEM, ANY],
        out_specs=[VMEM] * 8,
        scratch_shapes=[
            pltpu.VMEM((K, K), F32),
            pltpu.VMEM((K, K), BF16),
            pltpu.VMEM((K, K), BF16),
            pltpu.VMEM((LEG, K), F32),
            pltpu.VMEM((LEG * Q, K), F32),
            pltpu.VMEM((2, Q, K), F32),
            pltpu.VMEM((Q * 32, 128), F32),
            pltpu.VMEM((Q * 32, 128), F32),
            pltpu.SemaphoreType.DMA,
        ],
        compiler_params=pltpu.CompilerParams(vmem_limit_bytes=61 * MIB),
        name="measure",
    )(touched, spins, accept, site_ids, time_ids, left_proj, right_proj, weights, routing, perturb)
    here = [blocks[0]] + [None] * 7
    for d in FAR_FIRST:
        here[d] = lax.ppermute(blocks[d], ("zh", "c", "zl"), [(i, i ^ d) for i in range(8)])
    packed = pl.pallas_call(
        assemble_kernel,
        out_shape=[sds(tiles * 8, 128) for tiles in (77, 77, 8, 76, 76, 8)],
        in_specs=[VMEM] * 8,
        out_specs=[VMEM] * 6,
        compiler_params=pltpu.CompilerParams(vmem_limit_bytes=4 * MIB),
        name="assemble",
    )(*here)
    packed = [rows.reshape(-1, 8, 128) for rows in packed]
    one, two = gather_planes((packed[:3], packed[3:]))
    return pl.pallas_call(
        final_kernel,
        out_shape=sds(GQ, 128, SITES * LEG),
        in_specs=[VMEM] * 24 + [ANY],
        out_specs=ANY,
        scratch_shapes=[
            pltpu.VMEM((GQ, 128, 384), BF16),
            pltpu.VMEM((2, 128, CHUNK * 128), F32),
            pltpu.VMEM((2, 128, CHUNK * 128), F32),
            pltpu.SemaphoreType.DMA((4,)),
        ],
        compiler_params=pltpu.CompilerParams(vmem_limit_bytes=30 * MIB),
        name="accumulate",
    )(*one, *two, total)


def solution(mesh):
    cube = Mesh(mesh.devices.reshape(2, 2, 4, 4, 2), ("zh", "c", "x", "y", "zl"))
    grp, mem = ("zh", "c"), ("x", "y", "zl")
    both = grp + mem
    in_specs = (
        P(both, None, None),
        P(both, None, None),
        P(both, None, None),
        P(both, None, None),
        P(both, None),
        P(both, None),
        P(),
        P(),
        P(both),
        P(both, None),
        P(grp, mem, None),
    )
    return jax.shard_map(per_device, mesh=cube, in_specs=in_specs, out_specs=P(grp, mem, None), check_vma=False)
```

```python
import jax
import jax.numpy as jnp
import numpy as np
from jax import lax
from jax.experimental import pallas as pl
from jax.experimental.pallas import tpu as pltpu
from jax.sharding import Mesh
from jax.sharding import PartitionSpec as P


K = 1024
SITES = 64
LEG = 64
Q = 16
TIMES = 4096
UPDATES = 4
RANKB = 64
NS = UPDATES * RANKB
GQ = 4
RIGHT_ROWS = GQ * 32
LEFT_ROWS = GQ * 16
BLOCK_ROWS = RIGHT_ROWS + LEFT_ROWS + 8
F32 = jnp.float32
BF16 = jnp.bfloat16
NN = (((1,), (0,)), ((), ()))
NT = (((1,), (1,)), ((), ()))
TN = (((0,), (0,)), ((), ()))
MIB = 1 << 20


def mm(a, b, dims=NN):
    return lax.dot_general(a, b, dims, preferred_element_type=F32)


def split2(x):
    hi = x.astype(BF16)
    return hi, (x - hi.astype(F32)).astype(BF16)


def split3(x):
    hi = x.astype(BF16)
    rest = x - hi.astype(F32)
    mid = rest.astype(BF16)
    return hi, mid, (rest - mid.astype(F32)).astype(BF16)


def mm3(a, b, dims=NN):
    ah, al = a if isinstance(a, tuple) else split2(a)
    bh, bl = b if isinstance(b, tuple) else split2(b)
    rows = ah.shape[0]
    top = mm(jnp.concatenate([ah, al], axis=0), bh, dims)
    return top[:rows] + (top[rows:] + mm(ah, bl, dims))


def iota(shape, dim):
    return lax.broadcasted_iota(jnp.int32, shape, dim)


def row_to_column(row):
    n = row.shape[1]
    same = iota((n, n), 0) == iota((n, n), 1)
    return jnp.sum(jnp.where(same, row, jnp.zeros_like(row)), axis=1, keepdims=True)


def measure_kernel(
    chosen_ref, spin_ref, accept_ref, site_ref, time_ref, left_ref, right_ref, weight_ref, routing_ref, perturb_ref,
    *rest,
):
    outs = rest[:8]
    (matrix, p_hi, p_lo, polys, spread, vecs, left_meas, right_meas, sem) = rest[8:]
    load = pltpu.make_async_copy(perturb_ref.at[0], matrix, sem)
    load.start()

    abscissa = (2.0 * time_ref[...].astype(F32) + 1.0) / TIMES - 1.0
    before, now = jnp.ones_like(abscissa), abscissa
    polys[0:1, :] = before
    polys[1:2, :] = now * float(np.sqrt(3.0))
    for degree in range(1, LEG - 1):
        after = abscissa * now * ((2 * degree + 1) / (degree + 1)) - before * (degree / (degree + 1))
        before, now = now, after
        polys[degree + 1 : degree + 2, :] = now * float(np.sqrt(2.0 * degree + 3.0))

    sites = site_ref[...]
    onehot = (iota((SITES, K), 0) == sites).astype(F32).astype(BF16)
    onehot3 = jnp.concatenate([onehot, onehot, onehot], axis=0)
    for side, table_ref in ((0, left_ref), (1, right_ref)):
        table = jnp.concatenate(split3(table_ref[...]), axis=0)
        spread[...] = mm(table, onehot3, TN)
        total = jnp.zeros((Q, K), F32)
        for degree in range(LEG):
            total = total + spread[degree * Q : (degree + 1) * Q, :] * polys[degree : degree + 1, :]
        vecs[side] = total

    def one_row(values):
        return jnp.concatenate([values[u : u + 1, :] for u in range(UPDATES)], axis=1)

    chosen = row_to_column(one_row(chosen_ref[0].astype(F32))).astype(jnp.int32)
    pick = (iota((NS, K), 1) == chosen).astype(F32).astype(BF16)
    gamma = one_row(accept_ref[0].astype(F32) * jnp.where(spin_ref[0] == 1, 0.6, -0.4))
    gamma_column = row_to_column(gamma)
    load.wait()
    for step in range(4):
        rows = slice(step * 256, (step + 1) * 256)
        hi, lo = split2(matrix[rows, :])
        p_hi[rows, :] = hi
        p_lo[rows, :] = lo
    ph, plo = p_hi[...], p_lo[...]
    v, w = vecs[0], vecs[1]
    wh, wl = split2(w)
    high = mm(jnp.concatenate([pick, wh, wl], axis=0), ph)
    low = mm(jnp.concatenate([pick, wh], axis=0), plo)
    rows_hi, rows_lo = high[:NS].astype(BF16), low[:NS].astype(BF16)
    from_w = high[NS : NS + Q] + high[NS + Q :] + low[NS:]
    same = mm(pick, pick, NT)
    small = mm(rows_hi, pick, NT) + mm(rows_lo, pick, NT)
    vs = split3(v)
    p_vec = mm(pick, vs[0], NT) + mm(pick, vs[1], NT) + mm(pick, vs[2], NT)
    p_vec = p_vec + mm3((rows_hi, rows_lo), (vs[0], vs[1]), NT)
    fs = split3(from_w)
    q_vec = mm(fs[0], pick, NT) + mm(fs[1], pick, NT) + mm(fs[2], pick, NT)
    row_block = lax.div(iota((NS, NS), 0), RANKB)
    col_block = lax.div(iota((NS, NS), 1), RANKB)
    c_all, r_all = jnp.zeros((NS, NS), F32), jnp.zeros((NS, NS), F32)
    x, y = jnp.zeros((NS, Q), F32), jnp.zeros((Q, NS), F32)
    for update in range(UPDATES):
        mine = col_block == update
        columns = jnp.where(mine, small * gamma, 0.0)
        y_now = jnp.where(mine[:Q], q_vec * gamma, 0.0)
        rows_now = small + same
        x = jnp.where(row_block[:, :Q] == update, p_vec, x)
        y = y + y_now
        if update < UPDATES - 1:
            c_all = c_all + columns
            r_all = jnp.where(row_block == update, rows_now, r_all)
            half = slice(update // 2 * 128, update // 2 * 128 + 128)
            columns, y_now, rows_now = columns[:, half], y_now[:, half], split2(rows_now[half])
            change = mm3(jnp.concatenate([columns, y_now], axis=0), rows_now)
            p_vec = p_vec - mm3(columns, p_vec[half])
            small = small - change[:NS]
            q_vec = q_vec - change[NS:]
    lower = split2(jnp.where(row_block > col_block, c_all, 0.0))
    upper = split2(jnp.where(row_block < col_block, r_all, 0.0) * gamma)
    lower_twice, upper_twice = split2(mm3(lower, lower)), split2(mm3(upper, upper))
    z = x + mm3(upper_twice, x)
    y2 = y + mm3(y, lower_twice)
    z = z - mm3(upper, z)
    y2 = y2 - mm3(y2, lower)
    zs, ys = split3(z * gamma_column), split3(y2)
    left_arg = v - (mm(zs[0], pick, TN) + mm(zs[1], pick, TN) + mm(zs[2], pick, TN))
    ah, al = split2(left_arg)
    streamed = mm(ph, jnp.concatenate([ah, al], axis=0), NT)
    streamed = streamed[:, :Q] + (streamed[:, Q:] + mm(plo, ah, NT))
    left_image = v + streamed.T
    right_arg = w - (mm(ys[0], pick) + mm(ys[1], pick) + mm(ys[2], pick))
    right_image = right_arg + from_w - mm3((ys[0], ys[1]), (rows_hi, rows_lo))

    odd = lax.rem(sites, 2).astype(F32)
    values = polys[...]
    values = jnp.concatenate([values * (1.0 - odd), values * odd], axis=0)
    both = jnp.concatenate(split2(values), axis=0)
    pair = iota((32, K), 0) == lax.div(sites, 2)
    for image, meas in ((right_image, right_meas), (left_image, left_meas)):
        ih = image.astype(BF16).astype(F32)
        il = image - ih

        def masked(part):
            return jnp.concatenate(
                [jnp.where(pair, part[q : q + 1, :], 0.0).astype(BF16) for q in range(Q)], axis=0
            )

        high = mm(masked(ih), both, NT)
        low = mm(masked(il), both[:128], NT)
        meas[...] = high[:, :128] + (high[:, 128:] + low)

    lane = iota((8, 128), 1)
    own_group = lax.axis_index("zh") * 2 + lax.axis_index("c")
    key = (routing_ref[0, 0] + 32 * own_group).astype(F32)
    meta = jnp.where(lane == 0, weight_ref[0], jnp.where(lane == 1, key, 0.0))
    for distance in range(8):
        target = (own_group * 2 + lax.axis_index("zl")) ^ distance
        group, half = target // 2, target % 2
        first = pl.multiple_of(group * RIGHT_ROWS, RIGHT_ROWS)
        outs[distance][0:RIGHT_ROWS, :] = right_meas[pl.ds(first, RIGHT_ROWS), :]
        outs[distance][RIGHT_ROWS : RIGHT_ROWS + LEFT_ROWS, :] = left_meas[pl.ds(first + half, LEFT_ROWS, stride=2), :]
        outs[distance][RIGHT_ROWS + LEFT_ROWS :, :] = meta


TILE_META = 64
HALF = 32


def assemble_kernel(*refs):
    blocks, outs = refs[:8], (refs[8:11], refs[11:14])
    place = (lax.axis_index("x"), lax.axis_index("y"))
    for colour in range(2):
        up, down, own = outs[colour]
        size = 65 - colour
        for d in range(8):
            rows = blocks[d][colour * 64 : (colour + 1) * 64, :]
            for ref in (up, down):
                ref[pl.ds(d, 64, stride=8), :] = rows
                if colour == 0:
                    first = RIGHT_ROWS + LEFT_ROWS
                    ref[TILE_META * 8 + d : TILE_META * 8 + d + 1, :] = blocks[d][first : first + 1, :]

        def fill(ref, at, along, across):
            shift = (along, across) if colour == 0 else (across, along)
            owner = ((place[0] + shift[0]) % 4) * 4 + (place[1] + shift[1]) % 4
            for d in range(8):
                rows = blocks[d][pl.ds(RIGHT_ROWS + colour * 32 + owner, 2, stride=16), :]
                ref[pl.ds(at * 8 + d, 2, stride=8), :] = rows

        for across in range(4):
            fill(up, size + 2 * across, 1, across)
            fill(down, size + 2 * across, 3, across)
            fill(own, 2 * across, 0, across)
        for k in range(2):
            fill(up, size + 8 + 2 * k, 2, k)
            fill(down, size + 8 + 2 * k, 2, 2 + k)


CHUNK = 16
STEPS = 32 // CHUNK


def find_tiles(colour):
    n = 65 - colour
    P, OWN, A, B, C, D, E, F, G, H, I, J = range(12)
    right = {
        (0, 0): ((P, 0), (P, HALF)),
        (3, 0): ((A, 0), (A, HALF)),
        (1, 0): ((B, 0), (B, HALF)),
        (2, 0): ((C, 0), (D, 0)),
        (0, 2): ((I, 0), (I, HALF)),
        (3, 2): ((I, n), (J, 0)),
        (1, 2): ((J, n - HALF), (J, n)),
        (2, 2): ((I, n + HALF), (J, 2 * n - HALF)),
    }
    left = {
        (0, 0): (OWN, 0),
        (3, 0): (A, n),
        (1, 0): (B, n),
        (2, 0): (C, HALF),
        (0, 2): (I, n + 2 * HALF),
        (3, 2): (I, n + 2 * HALF + 2),
        (1, 2): (J, 3 * n - 2 * HALF),
        (2, 2): (J, 3 * n - 2 * HALF + 2),
    }
    for across, near, far in ((3, E, G), (1, F, H)):
        for i, along in enumerate((0, 3, 1)):
            right[along, across] = ((near, i * n), (near, i * n + HALF))
        right[2, across] = ((far, 0), (far, HALF))
        for i, along in enumerate((0, 3, 1, 2)):
            left[along, across] = (far, n + 2 * i)
    return right, left


PLACES = [(along, across) for across in (0, 1, 3, 2) for along in range(4)]
EARLY = 12
EARLY_ROWS = EARLY * 8


def right_rows(buffers, tiles, places, half, tile):
    chosen = [tiles[0][place][half] for place in places]
    return jnp.concatenate([buffers[which][first + tile] for which, first in chosen], axis=0)


def split_kernel(*refs):
    buffers, out = (refs[:10], refs[10:20]), refs[20]
    for q in range(GQ):
        tiles = find_tiles(q // 2)
        for j in range(32):
            hi, lo = split2(right_rows(buffers[q // 2], tiles, PLACES[:EARLY], q % 2, j))
            out[q, 0:EARLY_ROWS, j * 128 : (j + 1) * 128] = hi
            out[q, EARLY_ROWS : 2 * EARLY_ROWS, j * 128 : (j + 1) * 128] = lo


def final_kernel(*refs):
    buffers, early, total_ref, out_ref, l_top, results, sem = (refs[:12], refs[12:24]), *refs[24:]
    tiles = [find_tiles(colour) for colour in range(2)]
    diag = iota((128, 128), 0) == iota((128, 128), 1)
    for colour in range(2):
        metas = []
        for place in PLACES:
            which, first = tiles[0][0][place if colour == 0 else place[::-1]][1]
            metas.append(buffers[0][which][first + TILE_META - HALF])
        mine = jnp.concatenate(metas, axis=0)
        weight, key = mine[:, 0:1], mine[:, 1:2]
        key_row = jnp.sum(jnp.where(diag, key, 0.0), axis=0, keepdims=True)
        weight_row = jnp.sum(jnp.where(diag, weight, 0.0), axis=0, keepdims=True)
        own = jnp.sum(jnp.where(key == key_row, weight_row, 0.0), axis=1, keepdims=True)
        factors = weight / own
        for k in range(2):
            pairs = [tiles[colour][1][place] for place in PLACES]
            left = jnp.concatenate([buffers[colour][which][first + k] for which, first in pairs], axis=0)
            hi, lo = split2((left * factors).T)
            l_top[2 * colour + k] = jnp.concatenate([hi, lo, hi], axis=1)

    def store(step):
        q, n = step // STEPS, step % STEPS
        return pltpu.make_async_copy(
            results.at[step % 2], out_ref.at[q, :, pl.ds(n * CHUNK * 128, CHUNK * 128)], sem.at[step % 2]
        )

    for step in range(GQ * STEPS):
        q, n = step // STEPS, step % STEPS
        if step >= 2:
            store(step - 2).wait()
        for j in range(0, CHUNK, 2):
            tile = n * CHUNK + j
            there = slice(tile * 128, (tile + 2) * 128)
            late = jnp.concatenate(
                [right_rows(buffers[q // 2], tiles[q // 2], PLACES[EARLY:], q % 2, tile + k) for k in range(2)], axis=1
            )
            late_hi, late_lo = split2(late)
            hi = jnp.concatenate([early[q, 0:EARLY_ROWS, there], late_hi], axis=0)
            lo = jnp.concatenate([early[q, EARLY_ROWS : 2 * EARLY_ROWS, there], late_lo], axis=0)
            right3 = jnp.concatenate([hi, hi, lo], axis=0)
            results[step % 2, :, j * 128 : (j + 2) * 128] = total_ref[q, :, there] + mm(l_top[q], right3)
        store(step).start()
    for step in range(GQ * STEPS - 2, GQ * STEPS):
        store(step).wait()


ANY = pl.BlockSpec(memory_space=pl.ANY)
VMEM = pl.BlockSpec(memory_space=pltpu.VMEM)
SMEM = pl.BlockSpec(memory_space=pltpu.SMEM)


def sds(*shape):
    return jax.ShapeDtypeStruct(shape, F32)


UP = [(i, (i + 1) % 4) for i in range(4)]
DOWN = [(i, (i - 1) % 4) for i in range(4)]


FAR_FIRST = (4, 6, 5, 7, 1, 3, 2)


def hop(axis, way, *parts):
    value = jnp.concatenate(parts, axis=0) if len(parts) > 1 else parts[0]
    return lax.ppermute(value, axis, way)


def gather_planes(colours):
    axes = (("x", "y"), ("y", "x"))
    state = []
    for (first, _), (up, down, own) in zip(axes, colours):
        state.append([up, own, hop(first, UP, up), hop(first, DOWN, down)])
    for (first, _), found, size in zip(axes, state, (65, 64)):
        a, b = found[2], found[3]
        found.append(hop(first, UP, a[:HALF], a[size + 8 :]))
        found.append(hop(first, DOWN, b[HALF:size], b[size + 8 :]))
    for (_, second), found, size in zip(axes, state, (65, 64)):
        line = jnp.concatenate([found[0][:size], found[2][:size], found[3][:size]], axis=0)
        found.append(hop(second, UP, line))
        found.append(hop(second, DOWN, line))
    for (_, second), found, size in zip(axes, state, (65, 64)):
        _, own, a, b, c, d = found[:6]
        n = size
        opposite = [c[:HALF], d[: n - HALF]]
        up = [own[2:4], a[n + 2 : n + 4], b[n + 2 : n + 4], c[HALF + 2 : HALF + 4], own[4:6], a[n + 4 : n + 6]]
        down = [own[6:8], a[n + 6 : n + 8], b[n + 6 : n + 8], d[n - HALF + 2 :], b[n + 4 : n + 6], d[n - HALF : n - HALF + 2]]
        found.append(hop(second, UP, *opposite, *up))
        found.append(hop(second, DOWN, *opposite, *down))
    for (_, second), found, n in zip(axes, state, (65, 64)):
        e, f, g, h = found[6:10]
        cut = n + HALF
        found.append(hop(second, UP, e[:cut], g[:HALF], g[n + 8 :]))
        found.append(hop(second, DOWN, f[cut:], h[HALF:n], h[n + 8 :]))
    return state


def per_device(perturb, touched, spins, accept, site_ids, time_ids, left_proj, right_proj, weights, routing, total):
    blocks = pl.pallas_call(
        measure_kernel,
        out_shape=[sds(BLOCK_ROWS, 128)] * 8,
        in_specs=[VMEM] * 7 + [SMEM, SMEM, ANY],
        out_specs=[VMEM] * 8,
        scratch_shapes=[
            pltpu.VMEM((K, K), F32),
            pltpu.VMEM((K, K), BF16),
            pltpu.VMEM((K, K), BF16),
            pltpu.VMEM((LEG, K), F32),
            pltpu.VMEM((LEG * Q, K), F32),
            pltpu.VMEM((2, Q, K), F32),
            pltpu.VMEM((Q * 32, 128), F32),
            pltpu.VMEM((Q * 32, 128), F32),
            pltpu.SemaphoreType.DMA,
        ],
        compiler_params=pltpu.CompilerParams(vmem_limit_bytes=61 * MIB),
        name="measure",
    )(touched, spins, accept, site_ids, time_ids, left_proj, right_proj, weights, routing, perturb)
    here = [blocks[0]] + [None] * 7
    for d in FAR_FIRST:
        here[d] = lax.ppermute(blocks[d], ("zh", "c", "zl"), [(i, i ^ d) for i in range(8)])
    packed = pl.pallas_call(
        assemble_kernel,
        out_shape=[sds(tiles * 8, 128) for tiles in (77, 77, 8, 76, 76, 8)],
        in_specs=[VMEM] * 8,
        out_specs=[VMEM] * 6,
        compiler_params=pltpu.CompilerParams(vmem_limit_bytes=4 * MIB),
        name="assemble",
    )(*here)
    packed = [rows.reshape(-1, 8, 128) for rows in packed]
    one, two = gather_planes((packed[:3], packed[3:]))
    early = pl.pallas_call(
        split_kernel,
        out_shape=jax.ShapeDtypeStruct((GQ, 2 * EARLY_ROWS, SITES * LEG), BF16),
        in_specs=[VMEM] * 20,
        out_specs=VMEM,
        compiler_params=pltpu.CompilerParams(vmem_limit_bytes=4 * MIB),
        name="split",
    )(*one[:10], *two[:10])
    return pl.pallas_call(
        final_kernel,
        out_shape=sds(GQ, 128, SITES * LEG),
        in_specs=[VMEM] * 26,
        out_specs=ANY,
        scratch_shapes=[
            pltpu.VMEM((GQ, 128, 384), BF16),
            pltpu.VMEM((2, 128, CHUNK * 128), F32),
            pltpu.SemaphoreType.DMA((2,)),
        ],
        compiler_params=pltpu.CompilerParams(vmem_limit_bytes=20 * MIB),
        name="accumulate",
    )(*one, *two, early, total)


def solution(mesh):
    cube = Mesh(mesh.devices.reshape(2, 2, 4, 4, 2), ("zh", "c", "x", "y", "zl"))
    grp, mem = ("zh", "c"), ("x", "y", "zl")
    both = grp + mem
    in_specs = (
        P(both, None, None),
        P(both, None, None),
        P(both, None, None),
        P(both, None, None),
        P(both, None),
        P(both, None),
        P(),
        P(),
        P(both),
        P(both, None),
        P(grp, mem, None),
    )
    return jax.shard_map(per_device, mesh=cube, in_specs=in_specs, out_specs=P(grp, mem, None), check_vma=False)
```
